32 devices in a mesh: expert: 16 (over z, y, x), dp: 2 (over core).
Axes of the slice: x: 2, y: 2, z: 4, core: 2. Of those that a mesh axis runs over, the one named last changes fastest.
Arguments:
- tokens: bfloat16 [512, 7168], P('expert', 'dp'), may hold values from -6 to 6
- cotangent: bfloat16 [512, 7168], P('expert', 'dp'), may hold values from -6 to 6
- expert_ids: int32 [512, 8], P('expert'), may hold values from 0 to 15, all different within a row; in each aligned block of 32 rows (0 to 31, 32 to 63, ...) at most 32 rows name the same one
- route_weight: float32 [512, 8], P('expert'), may hold values from 0.1 to 1
- gate_weight: bfloat16 [16, 7168, 1024], P('expert', 'dp'), may hold values from -0.0625 to 0.0625
- up_weight: bfloat16 [16, 7168, 1024], P('expert', 'dp'), may hold values from -0.0625 to 0.0625
- down_weight: bfloat16 [16, 7168, 1024], P('expert', 'dp'), may hold values from -0.1875 to 0.1875
Outputs:
- mixed: bfloat16 [512, 7168], P('expert', 'dp')
- grad_tokens: bfloat16 [512, 7168], P('expert', 'dp')
The draws below stay inside these ranges and needn't reach their ends.
Inputs may be any that keep to these rules, and one draw needn't show every extreme that they name: `expert_ids`: each row names 8 different experts. In the rows of one device (aligned blocks of 32 rows) no expert is named more than 32 times, and in every draw some block names some expert exactly 32 times.
All inputs are finite; a program needn't handle non-finite values.
Results may differ from the reference program's by a relative error of at most 0.028.
Values may be sent and summed in bfloat16 or wider, within the bound.
No kernel may reach another device: no remote copies, remote signals or barrier semaphores. Data moves between devices by JAX's collectives and lax.ppermute only.
A program may use at most 64 MiB of HBM per device.

```python
import math
import jax
import jax.numpy as jnp
import numpy as np
from jax import lax

D = 7168
FF = 1024
K = 8
TOK_DEV = 32
EXPERTS = 16
CAP = 32
ROWS = 512
TOKENS = 512
N_EXPERT = 16
N_DP = 2


def block_scale(own_key, extent, shards, smallest, top_value):
    factor_of, own = 1.0, jax.random.fold_in(own_key, 6)
    for position, shards_of in shards:
        draws = jnp.exp(jax.random.uniform(jax.random.fold_in(own, position), (shards_of,), jnp.float32, smallest / len(shards), top_value / len(shards)))
        factor_of = factor_of * jnp.repeat(draws, extent[position] // shards_of).reshape([-1 if axis == position else 1 for axis in range(len(extent))])
    return factor_of


def assign_block(key, own, number, rows, amount, top, reach, lean):
    sequence = jax.random.permutation(key, amount)
    crowded, common = portions_of(amount, rows * top, reach, lean, True), portions_of(amount, rows * top, reach, lean, False)
    places = jnp.arange(amount)

    def named(tallies, offset_by):
        used = int((tallies > 0).sum())
        fixed = max(1, used // 4)
        moved = fixed + (places - fixed + offset_by * (used - fixed)) % max(1, amount - fixed)
        return jnp.zeros((amount,), jnp.int32).at[sequence[jnp.where(places < fixed, places, moved)]].set(jnp.asarray(tallies, jnp.int32))

    tallies = jnp.where(number % 4 == 0, named(crowded, number // 4), named(common, number - number // 4 - 1))
    mixed = jax.random.permutation(jax.random.fold_in(own, 3), amount)
    donor, sink = mixed[0:amount // 2 * 2:2], mixed[1:amount // 2 * 2:2]
    slack = jnp.minimum(tallies[donor] - 1, reach - tallies[sink]) // 2
    slack = jnp.where((donor == sequence[0]) | (sink == sequence[0]) | (tallies[sink] == 0), 0, jnp.maximum(slack, 0))
    moved = jax.random.randint(jax.random.fold_in(own, 4), (amount // 2,), 0, 1 << 20) % (slack + 1)
    tallies = tallies.at[donor].add(-moved).at[sink].add(moved)
    members = jnp.searchsorted(jnp.cumsum(tallies), jnp.arange(rows * top), side="right").astype(jnp.int32)
    table = members.reshape(top, rows).T
    table = table[jax.random.permutation(jax.random.fold_in(own, 1), rows)]
    offset_by = jax.random.randint(jax.random.fold_in(own, 2), (rows, 1), 0, top)
    return jnp.take_along_axis(table, (jnp.arange(top)[None, :] + offset_by) % top, axis=1)


def portions_of(count, total, reach, lean, full):
    portions = [(1 << 20) // math.isqrt(grade ** lean) + 1 for grade in range(1, count + 1)]
    largest = reach if full else min(reach, max(-(-total // count), total * portions[0] // sum(portions)))
    least = 1 if total - largest >= count - 1 else 0
    holding, rest = [largest] + [least] * (count - 1), total - largest - least * (count - 1)
    while rest > 0:
        candidates = [i for i in range(1, count) if holding[i] < largest] or [i for i in range(1, count) if holding[i] < reach]
        whole, remaining = sum([portions[i] for i in candidates]), rest
        for i in candidates:
            extra = min(reach - holding[i], max(1, remaining * portions[i] // whole), rest)
            holding[i] = holding[i] + extra
            rest = rest - extra
    return np.array(holding)


def scatter_about(rng, dims, width, limit, cuts=(), kind=jnp.bfloat16):
    entries = width * jax.random.normal(rng, dims, jnp.float32)
    if cuts:
        entries = entries * block_scale(rng, dims, cuts, -0.22, 0.18)
    return jnp.clip(entries, -limit, limit).astype(kind)


def setup_inputs(seed: int = 0) -> dict:
    key_list = jax.random.split(jax.random.key(seed), 8)
    tokens = scatter_about(key_list[0], (TOKENS, D), 1.0, 6.0, ((0, 16), (1, 2)))
    cotangent = scatter_about(key_list[1], (TOKENS, D), 1.0, 6.0, ((0, 16), (1, 2)))
    expert_ids_keys = jax.random.split(jax.random.fold_in(key_list[2], 1), TOKENS // TOK_DEV)
    expert_ids_turns = jax.random.permutation(jax.random.fold_in(key_list[2], 3), TOKENS // TOK_DEV)
    expert_ids = jax.vmap(lambda own, number: assign_block(jax.random.fold_in(key_list[2], 2), own, number, TOK_DEV, EXPERTS, K, CAP, 2))(expert_ids_keys, expert_ids_turns).reshape((TOKENS, K))
    route_weight = jnp.clip(0.1 + 0.9 * jax.random.uniform(key_list[3], (TOKENS, K), jnp.float32) ** block_scale(key_list[3], (TOKENS, K), ((0, 16),), -0.2, 0.2), 0.1, 1.0)
    gate_weight = scatter_about(key_list[4], (EXPERTS, D, FF), D ** -0.5, 0.0625, ((0, 16), (1, 2)))
    up_weight = scatter_about(key_list[5], (EXPERTS, D, FF), D ** -0.5, 0.0625, ((0, 16), (1, 2)))
    down_weight = scatter_about(key_list[6], (EXPERTS, D, FF), FF ** -0.5, 0.1875, ((0, 16), (1, 2)))
    return {"tokens": tokens, "cotangent": cotangent, "expert_ids": expert_ids, "route_weight": route_weight, "gate_weight": gate_weight, "up_weight": up_weight, "down_weight": down_weight}


def slot_targets(ids_block):
    flat_ids = ids_block.reshape(-1)
    onehot = (flat_ids[:, None] == jnp.arange(EXPERTS, dtype=jnp.int32)[None, :]).astype(jnp.int32)
    before = jnp.cumsum(onehot, axis=0) - onehot
    return (flat_ids * CAP + jnp.sum(before * onehot, axis=1)).astype(jnp.int32)


def place_rows(target, rows):
    return jnp.zeros((EXPERTS * CAP, D), rows.dtype).at[target].set(rows)


def pick_rows(source, target):
    return source[target]


def to_experts(buffer):
    return buffer.reshape(N_EXPERT, EXPERTS, CAP, D).transpose(1, 0, 2, 3).reshape(EXPERTS, ROWS, D)


def to_blocks(buffer):
    return buffer.reshape(EXPERTS, N_EXPERT, CAP, D).transpose(1, 0, 2, 3).reshape(N_EXPERT, EXPERTS * CAP, D)


def blocked(left_rows, weight):
    share_width = D // N_DP
    partials = jnp.einsum('rnc,ncf->nrf', left_rows.reshape(ROWS, N_DP, share_width).astype(jnp.float32),
                          weight.reshape(N_DP, share_width, FF).astype(jnp.float32))
    rounded = lax.optimization_barrier(partials.astype(jnp.bfloat16))
    return jnp.sum(rounded.astype(jnp.float32), axis=0)


def expert_pass(operands):
    routed_tokens, routed_grads, gate_w, up_w, down_w = operands
    gate_pre = blocked(routed_tokens, gate_w)
    up_pre = blocked(routed_tokens, up_w)
    sig_gate = jax.nn.sigmoid(gate_pre)
    hidden = (gate_pre * sig_gate * up_pre).astype(jnp.bfloat16)
    expert_out = jnp.einsum('rf,df->rd', hidden.astype(jnp.float32), down_w.astype(jnp.float32)).astype(jnp.bfloat16)
    hidden_grad = blocked(routed_grads, down_w)
    up_grad = (hidden_grad * gate_pre * sig_gate).astype(jnp.bfloat16)
    gate_grad = (hidden_grad * up_pre * sig_gate * (1.0 + gate_pre * (1.0 - sig_gate))).astype(jnp.bfloat16)
    slot_grad = (jnp.einsum('rf,df->rd', gate_grad.astype(jnp.float32), gate_w.astype(jnp.float32))
                 + jnp.einsum('rf,df->rd', up_grad.astype(jnp.float32), up_w.astype(jnp.float32))).astype(jnp.bfloat16)
    return expert_out, slot_grad


def reference(tokens, cotangent, expert_ids, route_weight, gate_weight, up_weight, down_weight):
    pair_count = TOK_DEV * K
    targets = jax.vmap(slot_targets)(expert_ids.reshape(N_EXPERT, TOK_DEV, K))
    weights = route_weight.reshape(N_EXPERT, pair_count)
    token_rows = jnp.repeat(tokens.reshape(N_EXPERT, TOK_DEV, D), K, axis=1)
    grad_rows = (weights[:, :, None] * jnp.repeat(cotangent.reshape(N_EXPERT, TOK_DEV, D).astype(jnp.float32), K, axis=1)).astype(jnp.bfloat16)
    routed_tokens = to_experts(jax.vmap(place_rows)(targets, token_rows))
    routed_grads = to_experts(jax.vmap(place_rows)(targets, grad_rows))
    expert_out, slot_grad = lax.map(expert_pass, (routed_tokens, routed_grads, gate_weight, up_weight, down_weight))
    got_out = jax.vmap(pick_rows)(to_blocks(expert_out), targets)
    got_grad = jax.vmap(pick_rows)(to_blocks(slot_grad), targets)
    mixed = jnp.sum((weights[:, :, None] * got_out.astype(jnp.float32)).reshape(N_EXPERT, TOK_DEV, K, D), axis=2)
    grad_tokens = jnp.sum(got_grad.astype(jnp.float32).reshape(N_EXPERT, TOK_DEV, K, D), axis=2)
    return mixed.reshape(TOKENS, D).astype(jnp.bfloat16), grad_tokens.reshape(TOKENS, D).astype(jnp.bfloat16)
```

```python
import jax
import jax.numpy as jnp
from jax import lax
from jax.sharding import PartitionSpec as P


def local(tokens, cotangent, expert_ids, route_weight, gate_weight, up_weight, down_weight):
    f32, bf16 = jnp.float32, jnp.bfloat16
    me = lax.axis_index("expert")
    gate_w = gate_weight[0]
    up_w = up_weight[0]
    down_w = down_weight[0]
    all_tokens = lax.all_gather(tokens, "expert", axis=0, tiled=True)
    all_cot = lax.all_gather(cotangent, "expert", axis=0, tiled=True)
    all_ids = lax.all_gather(expert_ids, "expert", axis=0, tiled=True)
    all_weight = lax.all_gather(route_weight, "expert", axis=0, tiled=True)
    chosen = all_ids == me
    weight = jnp.sum(jnp.where(chosen, all_weight, 0.0), axis=1, keepdims=True)
    named = jnp.any(chosen, axis=1, keepdims=True)
    gate_part = jnp.dot(all_tokens, gate_w, preferred_element_type=f32).astype(bf16)
    up_part = jnp.dot(all_tokens, up_w, preferred_element_type=f32).astype(bf16)
    hidden_part = (weight * jnp.dot(all_cot, down_w, preferred_element_type=f32)).astype(bf16)
    gate = lax.psum(gate_part, "dp").astype(f32)
    up = lax.psum(up_part, "dp").astype(f32)
    hidden_grad = lax.psum(hidden_part, "dp").astype(f32)
    sig = jax.nn.sigmoid(gate)
    hidden = (gate * sig * up).astype(bf16)
    up_grad = (hidden_grad * gate * sig).astype(bf16)
    gate_grad = (hidden_grad * up * sig * (1.0 + gate * (1.0 - sig))).astype(bf16)
    contract = (((1,), (1,)), ((), ()))
    out = (weight * lax.dot_general(hidden, down_w, contract, preferred_element_type=f32)).astype(bf16)
    grad = (
        lax.dot_general(gate_grad, gate_w, contract, preferred_element_type=f32)
        + lax.dot_general(up_grad, up_w, contract, preferred_element_type=f32)
    )
    grad = jnp.where(named, grad, 0.0).astype(bf16)
    mixed = lax.psum_scatter(out, "expert", scatter_dimension=0, tiled=True)
    grad_tokens = lax.psum_scatter(grad, "expert", scatter_dimension=0, tiled=True)
    return (mixed, grad_tokens)


def solution(mesh):
    return jax.shard_map(
        local,
        mesh=mesh,
        in_specs=(
            P("expert", "dp"),
            P("expert", "dp"),
            P("expert", None),
            P("expert", None),
            P("expert", "dp", None),
            P("expert", "dp", None),
            P("expert", "dp", None),
        ),
        out_specs=(P("expert", "dp"), P("expert", "dp")),
        check_vma=False,
    )
```

```python
import jax
import jax.numpy as jnp
from jax import lax
from jax.sharding import PartitionSpec as P

F32, BF16 = jnp.float32, jnp.bfloat16


def folded(size):
    return list(range(0, 1)) + list(range(1, size, 2)) + list(range(2, size, 2))[::-1]


class Grid:
    def __init__(self, size):
        assert size % 4 == 0
        self.rings = size // 4
        order = folded(self.rings)
        step = {a: order[(i + 1) % self.rings] for i, a in enumerate(order)}
        self.along = [(e, step[e // 4] * 4 + e % 4) for e in range(size)]
        self.x = [(e, e ^ 1) for e in range(size)]
        self.y = [(e, e ^ 2) for e in range(size)]


def send(value, pairs):
    return lax.ppermute(value, "expert", pairs)


def gather(grid, block):
    blocks = [block]
    for _ in range(grid.rings - 1):
        blocks.append(send(blocks[-1], grid.along))
    half = block.shape[1] // 2
    left = jnp.concatenate([b[:, :half] for b in blocks], axis=0)
    right = jnp.concatenate([b[:, half:] for b in blocks], axis=0)
    left_x = send(left, grid.x)
    right_y = send(right, grid.y)
    left_y = send(left, grid.y)
    right_x = send(right, grid.x)
    left_xy = send(left_x, grid.y)
    right_xy = send(right_y, grid.x)
    halves = ((left, right), (left_x, right_x), (left_y, right_y), (left_xy, right_xy))
    return jnp.concatenate([jnp.concatenate(h, axis=1) for h in halves], axis=0)


def scatter(grid, product):
    x_bit, y_bit, both = 1, 2, 3
    sent_left = product((both, y_bit), 0)
    sent_right = product((both, x_bit), 1)
    got_left = send(sent_left.astype(BF16), grid.y)
    got_right = send(sent_right.astype(BF16), grid.x)
    kept_left = product((x_bit, 0), 0)
    kept_right = product((y_bit, 0), 1)
    rows = kept_left.shape[0] // 2
    sum_left = kept_left.astype(F32) + got_left.astype(F32)
    sum_right = kept_right.astype(F32) + got_right.astype(F32)
    got_left = send(sum_left[:rows].astype(BF16), grid.x)
    got_right = send(sum_right[:rows].astype(BF16), grid.y)
    total = jnp.concatenate(
        [sum_left[rows:] + got_left.astype(F32), sum_right[rows:] + got_right.astype(F32)], axis=1
    )
    block = rows // grid.rings
    running = total[block : 2 * block] if grid.rings > 1 else total[:block]
    for place in range(2, grid.rings + 1):
        place = place % grid.rings
        got = send(running.astype(BF16), grid.along).astype(F32)
        running = got + total[place * block : (place + 1) * block]
    return running.astype(BF16)


def local(tokens, cotangent, expert_ids, route_weight, gate_weight, up_weight, down_weight):
    experts = lax.axis_size("expert")
    shares = lax.axis_size("dp")
    grid = Grid(experts)
    me = lax.axis_index("expert")
    width = tokens.shape[1]
    names = jnp.arange(experts, dtype=jnp.int32)
    named = expert_ids[:, :, None] == names[None, None, :]
    table = jnp.sum(jnp.where(named, route_weight[:, :, None], 0.0), axis=1)
    high = lax.reduce_precision(table, 8, 7)
    low = table - high
    lanes = 128
    extra = jnp.concatenate([high, low], axis=1).astype(BF16)
    pad = -(2 * experts) % (2 * lanes)
    extra = jnp.pad(extra, ((0, 0), (0, pad)))
    lead = extra.shape[1] // 2
    all_rows = gather(grid, jnp.concatenate([extra, tokens], axis=1))
    all_cot = gather(grid, cotangent)
    all_tokens = all_rows[:, 2 * lead :]
    mine = (jnp.arange(2 * experts) % experts) == me
    weight = jnp.sum(
        jnp.where(mine[None, :], all_rows[:, : 2 * experts].astype(F32), 0.0), axis=1, keepdims=True
    )
    gate_w = gate_weight[0]
    up_w = up_weight[0]
    down_w = down_weight[0]

    def add_shares(rows, w, scale, after):
        if shares != 2 and after is not None:
            rows, after = lax.optimization_barrier((rows, after))
        part = jnp.dot(rows, w, preferred_element_type=F32)
        part = (part if scale is None else scale * part).astype(BF16)
        if shares == 2:
            return part.astype(F32) + lax.ppermute(part, "dp", [(0, 1), (1, 0)]).astype(F32), after
        return lax.psum(part, "dp"), after

    gate, _ = add_shares(all_tokens, gate_w, None, None)
    up, gate = add_shares(all_tokens, up_w, None, gate)
    hidden_grad, up = add_shares(lax.optimization_barrier(all_cot), down_w, weight, up)
    gate, up, hidden_grad = gate.astype(F32), up.astype(F32), hidden_grad.astype(F32)
    sig = jax.nn.sigmoid(gate)
    hidden = (gate * sig * up).astype(BF16)
    up_grad = (hidden_grad * gate * sig).astype(BF16)
    gate_grad = (hidden_grad * up * sig * (1.0 + gate * (1.0 - sig))).astype(BF16)
    contract = (((1,), (1,)), ((), ()))
    quarter = all_tokens.shape[0] // 4
    half = width // 2

    def rows_of(value, quarters):
        return jnp.concatenate([value[q * quarter : (q + 1) * quarter] for q in quarters], axis=0)

    def back(value, w, quarters, side):
        return lax.dot_general(
            rows_of(value, quarters), w[side * half : (side + 1) * half], contract,
            preferred_element_type=F32,
        )

    def out_part(quarters, side):
        return (rows_of(weight, quarters) * back(hidden, down_w, quarters, side)).astype(BF16)

    def grad_part(quarters, side):
        total = back(gate_grad, gate_w, quarters, side) + back(up_grad, up_w, quarters, side)
        return jnp.where(rows_of(weight, quarters) > 0.0, total, 0.0).astype(BF16)

    mixed = scatter(grid, out_part)
    grad_tokens = scatter(grid, grad_part)
    return (mixed, grad_tokens)


def solution(mesh):
    return jax.shard_map(
        local,
        mesh=mesh,
        in_specs=(
            P("expert", "dp"),
            P("expert", "dp"),
            P("expert", None),
            P("expert", None),
            P("expert", "dp", None),
            P("expert", "dp", None),
            P("expert", "dp", None),
        ),
        out_specs=(P("expert", "dp"), P("expert", "dp")),
        check_vma=False,
    )
```

```python
import jax
import jax.numpy as jnp
from jax import lax
from jax.experimental import pallas as pl
from jax.experimental.pallas import tpu as pltpu
from jax.sharding import PartitionSpec as P

F32, BF16 = jnp.float32, jnp.bfloat16
HERE, X, Y, XY = 0, 1, 2, 3
LANES = 128


class Grid:
    def __init__(self, size):
        assert size % 4 == 0
        self.rings = rings = size // 4
        self.size = size
        self.x = [(e, e ^ 1) for e in range(size)]
        self.y = [(e, e ^ 2) for e in range(size)]
        places = list(range(rings))
        cut = (rings + 1) // 2
        leaving = places[1:] + places[:1]
        self.leaving = [leaving[:cut], leaving[cut:]]

    def on(self, steps):
        return [(e, (e + 4 * steps) % self.size) for e in range(self.size)]


def send(value, pairs, axis="expert"):
    return lax.ppermute(value, axis, pairs)


def rows(*parts):
    return jnp.concatenate(parts, axis=0) if len(parts) > 1 else parts[0]


def around(grid, block):
    blocks = [block]
    for i in range(1, grid.rings):
        blocks.append(send(block, grid.on(i)))
    return blocks


def gather_by_place(grid, block):
    parts = []
    for p, here in enumerate(around(grid, block)):
        over_y = send(here, grid.y)
        over_x = send(here, grid.x)
        if p % 2:
            over_xy = send(over_y, grid.x)
        else:
            over_xy = send(over_x, grid.y)
        parts.append((here, over_x, over_y, over_xy))
    return parts


def gather_ring_first(grid, block):
    here = rows(*around(grid, block))
    over_x = send(here, grid.x)
    over_y = send(here, grid.y)
    over_xy = send(over_y, grid.x)
    return here, over_x, over_y, over_xy


def gather_ring_last(grid, block):
    over_y = send(block, grid.y)
    over_x = send(block, grid.x)
    over_xy = send(over_y, grid.x)
    return around(grid, rows(block, over_x, over_y, over_xy))


class Piece:
    def __init__(self, source, row, count, shift, width, first=0, column=0):
        self.source, self.row, self.count = source, row, count
        self.shift, self.width, self.first, self.column = shift, width, first, column


def fused_dot(arrays, pieces, height, width, weights, tail, scale):
    columns = weights[0].shape[1]
    step = 512
    per = columns // step
    count = len(arrays)
    masked = tail is not None
    tail_pieces = [
        Piece(p.source, p.row, p.count, 0, LANES, p.first, width) for p in pieces
    ] if masked else []
    moves = pieces + tail_pieces

    def kernel(*refs):
        sources = refs[:count]
        w_refs = refs[count : count + len(weights)]
        extra = refs[count + len(weights)]
        out = refs[count + len(weights) + 1]
        rest = refs[count + len(weights) + 2 :]
        if masked:
            sums, full, ends, sem = rest
        else:
            full, sem = rest
        at = pl.program_id(0)

        @pl.when(at == 0)
        def _():
            copies = []
            for i, p in enumerate(moves):
                target = full if i < len(pieces) else ends
                copies.append(
                    pltpu.make_async_copy(
                        sources[p.source].at[
                            pl.ds(p.first, p.count), pl.ds(p.column, p.width)
                        ],
                        target.at[pl.ds(p.row, p.count), pl.ds(p.shift, p.width)],
                        sem.at[i],
                    )
                )
            for c in copies:
                c.start()
            for c in copies:
                c.wait()
            if masked:
                value = ends[...].astype(F32) * extra[...]
                sums[...] = jnp.broadcast_to(
                    jnp.sum(value, axis=1, keepdims=True), sums.shape
                )

        for i, w in enumerate(w_refs):

            @pl.when(at // per == i)
            def _(w=w):
                part = jnp.dot(full[...], w[...], preferred_element_type=F32)
                if not masked:
                    part = part * extra[:, :1]
                out[...] = part.astype(BF16)

    weights = [pltpu.with_memory_space_constraint(w, pltpu.HBM) for w in weights]

    def w_map(i):
        return lambda at: (0, jnp.clip(at - i * per, 0, per - 1))

    extra = tail if masked else scale
    out_shape = [jax.ShapeDtypeStruct((height, columns * len(weights)), BF16)]
    out_specs = [pl.BlockSpec((height, step), lambda at: (0, at))]
    scratch = [pltpu.VMEM((height, width), BF16)]
    if masked:
        out_shape.append(jax.ShapeDtypeStruct((height, LANES), F32))
        out_specs.append(pl.BlockSpec((height, LANES), lambda at: (0, 0)))
        scratch.append(pltpu.VMEM((height, LANES), BF16))
    scratch.append(pltpu.SemaphoreType.DMA((len(moves),)))
    flops = 2 * height * width * columns * len(weights)
    moved = 2 * (width * columns * len(weights) + height * width + height * columns)
    return pl.pallas_call(
        kernel,
        grid=(per * len(weights),),
        in_specs=[pl.BlockSpec(memory_space=pl.ANY)] * count
        + [pl.BlockSpec((width, step), w_map(i)) for i in range(len(weights))]
        + [pl.BlockSpec(extra.shape, lambda at: (0, 0))],
        out_specs=out_specs,
        out_shape=out_shape,
        scratch_shapes=scratch,
        compiler_params=pltpu.CompilerParams(
            dimension_semantics=("arbitrary",), vmem_limit_bytes=26 << 20
        ),
        cost_estimate=pl.CostEstimate(flops=flops, bytes_accessed=moved, transcendentals=0),
    )(*arrays, *weights, extra)


def plus(value, got):
    return value.astype(F32) + got.astype(F32)


def scatter_around(grid, blocks):
    total = blocks[0]
    for i in range(1, grid.rings):
        total = plus(total, send(blocks[i].astype(BF16), grid.on(-i)))
    return total.astype(BF16)


def pairs(quarters, places):
    return [(q, p) for q in quarters for p in places]


def scatter_ring_last(grid, product):
    places = range(grid.rings)
    sent = product(pairs((XY, Y), places))
    got = send(sent, grid.y)
    total = plus(product(pairs((X, HERE), places)), got)
    size = total.shape[0] // 2
    got = send(total[:size].astype(BF16), grid.x)
    total = plus(total[size:], got)
    size //= grid.rings
    return scatter_around(grid, [total[p * size : (p + 1) * size] for p in places])


def scatter_ring_first(grid, product):
    blocks = {}
    for places in grid.leaving:
        part = product([(q, p) for p in places for q in (XY, X, Y, HERE)])
        size = part.shape[0] // max(1, len(places))
        for i, p in enumerate(places):
            blocks[p] = part[i * size : (i + 1) * size]
    plane = scatter_around(grid, blocks)
    size = plane.shape[0] // 4
    xy, x, y, here = [plane[q * size : (q + 1) * size] for q in range(4)]
    got = send(rows(xy, x), grid.x)
    over_y = plus(y, got[:size]).astype(BF16)
    here = plus(here, got[size:])
    got = send(over_y, grid.y)
    return plus(here, got).astype(BF16)


def scatter_two_ways(grid, product):
    groups = [g for g in grid.leaving if g]

    def split(value):
        size = value.shape[0] // grid.rings
        ends = [size * sum(len(h) for h in groups[:i]) for i in range(len(groups) + 1)]
        return [value[a:b] for a, b in zip(ends, ends[1:])]

    def part(quarters, side):
        return split(product([qp for g in groups for qp in pairs(quarters, g)], side))

    sent_left = part((XY, Y), 0)
    sent_right = part((XY, X), 1)
    got_left, got_right = [], []
    for g in range(len(groups)):
        got_left.append(send(sent_left[g], grid.y))
        got_right.append(send(sent_right[g], grid.x))
    kept_left = lax.optimization_barrier(part((X, HERE), 0))
    kept_right = lax.optimization_barrier(part((Y, HERE), 1))
    blocks = {}
    for g, places in enumerate(groups):
        left = plus(kept_left[g], got_left[g])
        right = plus(kept_right[g], got_right[g])
        size = left.shape[0] // 2
        over_x = send(left[:size].astype(BF16), grid.x)
        over_y = send(right[:size].astype(BF16), grid.y)
        total = jnp.concatenate([plus(left[size:], over_x), plus(right[size:], over_y)], axis=1)
        size //= len(places)
        for i, p in enumerate(places):
            blocks[p] = total[i * size : (i + 1) * size]
    return scatter_around(grid, blocks)


def native(tokens, cotangent, expert_ids, route_weight, gate_weight, up_weight, down_weight):
    me = lax.axis_index("expert")
    gate_w, up_w, down_w = gate_weight[0], up_weight[0], down_weight[0]
    all_tokens = lax.all_gather(tokens, "expert", axis=0, tiled=True)
    all_cot = lax.all_gather(cotangent, "expert", axis=0, tiled=True)
    all_ids = lax.all_gather(expert_ids, "expert", axis=0, tiled=True)
    all_weight = lax.all_gather(route_weight, "expert", axis=0, tiled=True)
    weight = jnp.sum(jnp.where(all_ids == me, all_weight, 0.0), axis=1, keepdims=True)
    gate_part = jnp.dot(all_tokens, gate_w, preferred_element_type=F32).astype(BF16)
    up_part = jnp.dot(all_tokens, up_w, preferred_element_type=F32).astype(BF16)
    grad_part = (weight * jnp.dot(all_cot, down_w, preferred_element_type=F32)).astype(BF16)
    gate = lax.psum(gate_part, "dp").astype(F32)
    up = lax.psum(up_part, "dp").astype(F32)
    hidden_grad = lax.psum(grad_part, "dp").astype(F32)
    sig = jax.nn.sigmoid(gate)
    hidden = (gate * sig * up).astype(BF16)
    up_grad = (hidden_grad * gate * sig).astype(BF16)
    gate_grad = (hidden_grad * up * sig * (1.0 + gate * (1.0 - sig))).astype(BF16)
    contract = (((1,), (1,)), ((), ()))
    out = lax.dot_general(hidden, down_w, contract, preferred_element_type=F32)
    grad = lax.dot_general(gate_grad, gate_w, contract, preferred_element_type=F32)
    grad += lax.dot_general(up_grad, up_w, contract, preferred_element_type=F32)
    return tuple(
        lax.psum_scatter(v.astype(BF16), "expert", scatter_dimension=0, tiled=True)
        for v in (weight * out, grad)
    )


def local(tokens, cotangent, expert_ids, route_weight, gate_weight, up_weight, down_weight):
    experts = lax.axis_size("expert")
    shares = lax.axis_size("dp")
    size, width = tokens.shape
    short = experts % 4 == 0 and experts // 4 <= 4 and 2 * experts <= LANES
    if not (short and shares == 2 and width % (2 * LANES) == 0 and size % 16 == 0):
        return native(
            tokens, cotangent, expert_ids, route_weight, gate_weight, up_weight, down_weight
        )
    grid = Grid(experts)
    me = lax.axis_index("expert")
    half = width // 2
    names = jnp.arange(experts, dtype=jnp.int32)
    named = expert_ids[:, :, None] == names[None, None, :]
    table = jnp.sum(jnp.where(named, route_weight[:, :, None], 0.0), axis=1)
    high = lax.reduce_precision(table, 8, 7)
    extra = jnp.concatenate([high, table - high], axis=1).astype(BF16)
    extra = jnp.pad(extra, ((0, 0), (0, -(2 * experts) % LANES)))
    block = jnp.concatenate([tokens, extra], axis=1)
    parts = gather_by_place(grid, block)
    by_quarter = gather_ring_first(grid, cotangent[:, :half])
    by_place = gather_ring_last(grid, cotangent[:, half:])
    gate_w = gate_weight[0]
    up_w = up_weight[0]
    down_w = down_weight[0]
    lanes = jnp.arange(extra.shape[1])[None, :]
    mine = ((lanes % experts) == me) & (lanes < 2 * experts)
    height = experts * size
    token_arrays, token_pieces = [], []
    cot_arrays = list(by_quarter) + by_place
    cot_pieces = []
    for q in range(4):
        cot_pieces.append(Piece(q, q * grid.rings * size, grid.rings * size, 0, half))
        for p in range(grid.rings):
            row = (q * grid.rings + p) * size
            token_pieces.append(Piece(len(token_arrays), row, size, 0, width))
            token_arrays.append(parts[p][q])
            cot_pieces.append(Piece(4 + p, row, size, half, width - half, q * size))

    def share_sum(part):
        return plus(part, send(part, [(0, 1), (1, 0)], "dp"))

    both, weight = fused_dot(
        token_arrays, token_pieces, height, width, [gate_w, up_w], mine.astype(F32), None
    )
    weight = weight[:, :1]
    both = share_sum(both)
    gate, up = both[:, : gate_w.shape[1]], both[:, gate_w.shape[1] :]
    sig = jax.nn.sigmoid(gate)
    hidden = (weight * (gate * sig * up)).astype(BF16)
    hidden, scale = lax.optimization_barrier((hidden, weight))
    (part,) = fused_dot(cot_arrays, cot_pieces, height, width, [down_w], None, scale)
    hidden_grad = share_sum(part)
    up_grad = (hidden_grad * gate * sig).astype(BF16)
    gate_grad = (hidden_grad * up * sig * (1.0 + gate * (1.0 - sig))).astype(BF16)
    contract = (((1,), (1,)), ((), ()))

    def rows_of(value, which):
        runs = []
        for q, p in which:
            start = (q * grid.rings + p) * size
            if runs and runs[-1][1] == start:
                runs[-1][1] = start + size
            else:
                runs.append([start, start + size])
        return rows(*[value[a:b] for a, b in runs])

    def back(value, w, which, side):
        return lax.dot_general(
            rows_of(value, which), w[side * half : (side + 1) * half], contract,
            preferred_element_type=F32,
        )

    def out_part(which, side):
        return back(hidden, down_w, which, side).astype(BF16)

    def grad_part(which, side):
        total = back(gate_grad, gate_w, which, side) + back(up_grad, up_w, which, side)
        return total.astype(BF16)

    mixed = jnp.concatenate(
        [
            scatter_ring_last(grid, lambda which: out_part(which, 0)),
            scatter_ring_first(grid, lambda which: out_part(which, 1)),
        ],
        axis=1,
    )
    grad_tokens = scatter_two_ways(grid, grad_part)
    return (mixed, grad_tokens)


def solution(mesh):
    return jax.shard_map(
        local,
        mesh=mesh,
        in_specs=(
            P("expert", "dp"),
            P("expert", "dp"),
            P("expert", None),
            P("expert", None),
            P("expert", "dp", None),
            P("expert", "dp", None),
            P("expert", "dp", None),
        ),
        out_specs=(P("expert", "dp"), P("expert", "dp")),
        check_vma=False,
    )
```

```python
import jax
import jax.numpy as jnp
from jax import lax
from jax.experimental import pallas as pl
from jax.experimental.pallas import tpu as pltpu
from jax.sharding import PartitionSpec as P

F32, BF16 = jnp.float32, jnp.bfloat16
HERE, X, Y, XY = 0, 1, 2, 3
LANES = 128


class Grid:
    def __init__(self, size):
        assert size % 4 == 0
        self.rings = rings = size // 4
        self.size = size
        self.order = [0] + list(range(1, rings, 2)) + list(range(2, rings, 2))[::-1]
        self.x = [(e, e ^ 1) for e in range(size)]
        self.y = [(e, e ^ 2) for e in range(size)]
        places = list(range(rings))
        cut = (rings + 1) // 2
        leaving = places[1:] + places[:1]
        self.leaving = [leaving[:cut], leaving[cut:]]
        self.single = [[p] for p in places]
        self.together = [leaving]

    def on(self, steps):
        order = self.order
        to = {a: order[(i + steps) % self.rings] for i, a in enumerate(order)}
        return [(e, to[e // 4] * 4 + e % 4) for e in range(self.size)]


def send(value, pairs, axis="expert"):
    return lax.ppermute(value, axis, pairs)


def rows(*parts):
    return jnp.concatenate(parts, axis=0) if len(parts) > 1 else parts[0]


def around(grid, block, ring):
    blocks = [block]
    for i in range(1, grid.rings):
        source, steps = (blocks[-1], 1) if ring else (block, i)
        blocks.append(send(source, grid.on(steps)))
    return blocks


def gather(grid, block, groups, ring):
    blocks = around(grid, block, ring)
    parts = []
    for g, places in enumerate(groups):
        here = rows(*[blocks[p] for p in places])
        over_y = send(here, grid.y)
        over_x = send(here, grid.x)
        if g % 2:
            over_xy = send(over_y, grid.x)
        else:
            over_xy = send(over_x, grid.y)
        parts.append((here, over_x, over_y, over_xy))
    return parts


class Piece:
    def __init__(self, source, row, count, shift, width, first=0, column=0):
        self.source, self.row, self.count = source, row, count
        self.shift, self.width, self.first, self.column = shift, width, first, column


def assemble(arrays, pieces, height, width, mask):
    count = len(arrays)
    masked = mask is not None
    moves = list(pieces)
    if masked:
        moves += [Piece(p.source, p.row, p.count, 0, LANES, p.first, width) for p in pieces]

    def kernel(*refs):
        sources = refs[:count]
        if masked:
            mask_ref, full, sums, ends, sem = refs[count:]
        else:
            full, sem = refs[count:]
        copies = []
        for i, p in enumerate(moves):
            target = full if i < len(pieces) else ends
            copies.append(
                pltpu.make_async_copy(
                    sources[p.source].at[pl.ds(p.first, p.count), pl.ds(p.column, p.width)],
                    target.at[pl.ds(p.row, p.count), pl.ds(p.shift, p.width)],
                    sem.at[i],
                )
            )
        for c in copies:
            c.start()
        for c in copies:
            c.wait()
        if masked:
            value = ends[...].astype(F32) * mask_ref[...]
            sums[...] = jnp.broadcast_to(jnp.sum(value, axis=1, keepdims=True), sums.shape)

    out_shape = [jax.ShapeDtypeStruct((height, width), BF16)]
    scratch = [pltpu.SemaphoreType.DMA((len(moves),))]
    if masked:
        out_shape.append(jax.ShapeDtypeStruct((height, LANES), F32))
        scratch.insert(0, pltpu.VMEM((height, LANES), BF16))
    vmem = pl.BlockSpec(memory_space=pltpu.VMEM)
    return pl.pallas_call(
        kernel,
        in_specs=[pl.BlockSpec(memory_space=pl.ANY)] * count + [vmem] * masked,
        out_specs=[vmem] * len(out_shape),
        out_shape=out_shape,
        scratch_shapes=scratch,
        compiler_params=pltpu.CompilerParams(vmem_limit_bytes=12 << 20),
        cost_estimate=pl.CostEstimate(
            flops=0, bytes_accessed=4 * height * width, transcendentals=0
        ),
    )(*arrays, *([mask] if masked else []))


def plus(value, got):
    return value.astype(F32) + got.astype(F32)


def scatter_around(grid, blocks):
    near = (grid.rings - 1) // 2
    total, sent = blocks[0], 0
    for path, steps in ((range(near, 0, -1), -1), (range(near + 1, grid.rings), 1)):
        running = None
        for i in path:
            running = blocks[i] if running is None else plus(blocks[i], running)
            sent += 1
            running = send(running.astype(BF16), grid.on(steps))
        if running is not None:
            total = plus(total, running)
    return total.astype(BF16)


def pairs(quarters, places):
    return [(q, p) for q in quarters for p in places]


def scatter(grid, product, groups):

    def split(value):
        size = value.shape[0] // grid.rings
        ends = [size * sum(len(h) for h in groups[:i]) for i in range(len(groups) + 1)]
        return [value[a:b] for a, b in zip(ends, ends[1:])]

    def part(quarters, side):
        return split(product([qp for g in groups for qp in pairs(quarters, g)], side))

    sent_left = part((XY, Y), 0)
    sent_right = part((XY, X), 1)
    got_left, got_right = [], []
    for g in range(len(groups)):
        got_left.append(send(sent_left[g], grid.y))
        got_right.append(send(sent_right[g], grid.x))
    kept_left = [lax.optimization_barrier(k) for k in part((X, HERE), 0)]
    kept_right = [lax.optimization_barrier(k) for k in part((Y, HERE), 1)]
    blocks = {}
    for g, places in enumerate(groups):
        left = plus(kept_left[g], got_left[g])
        right = plus(kept_right[g], got_right[g])
        size = left.shape[0] // 2
        sent_left = left[:size].astype(BF16)
        sent_right = right[:size].astype(BF16)
        over_x = send(sent_left, grid.x)
        over_y = send(sent_right, grid.y)
        total = jnp.concatenate([plus(left[size:], over_x), plus(right[size:], over_y)], axis=1)
        size //= len(places)
        for i, p in enumerate(places):
            blocks[p] = total[i * size : (i + 1) * size]
    return scatter_around(grid, blocks)


def native(tokens, cotangent, expert_ids, route_weight, gate_weight, up_weight, down_weight):
    me = lax.axis_index("expert")
    gate_w, up_w, down_w = gate_weight[0], up_weight[0], down_weight[0]
    all_tokens = lax.all_gather(tokens, "expert", axis=0, tiled=True)
    all_cot = lax.all_gather(cotangent, "expert", axis=0, tiled=True)
    all_ids = lax.all_gather(expert_ids, "expert", axis=0, tiled=True)
    all_weight = lax.all_gather(route_weight, "expert", axis=0, tiled=True)
    weight = jnp.sum(jnp.where(all_ids == me, all_weight, 0.0), axis=1, keepdims=True)
    gate_part = jnp.dot(all_tokens, gate_w, preferred_element_type=F32).astype(BF16)
    up_part = jnp.dot(all_tokens, up_w, preferred_element_type=F32).astype(BF16)
    grad_part = (weight * jnp.dot(all_cot, down_w, preferred_element_type=F32)).astype(BF16)
    gate = lax.psum(gate_part, "dp").astype(F32)
    up = lax.psum(up_part, "dp").astype(F32)
    hidden_grad = lax.psum(grad_part, "dp").astype(F32)
    sig = jax.nn.sigmoid(gate)
    hidden = (gate * sig * up).astype(BF16)
    up_grad = (hidden_grad * gate * sig).astype(BF16)
    gate_grad = (hidden_grad * up * sig * (1.0 + gate * (1.0 - sig))).astype(BF16)
    contract = (((1,), (1,)), ((), ()))
    out = lax.dot_general(hidden, down_w, contract, preferred_element_type=F32)
    grad = lax.dot_general(gate_grad, gate_w, contract, preferred_element_type=F32)
    grad += lax.dot_general(up_grad, up_w, contract, preferred_element_type=F32)
    return tuple(
        lax.psum_scatter(v.astype(BF16), "expert", scatter_dimension=0, tiled=True)
        for v in (weight * out, grad)
    )


def local(tokens, cotangent, expert_ids, route_weight, gate_weight, up_weight, down_weight):
    experts = lax.axis_size("expert")
    shares = lax.axis_size("dp")
    size, width = tokens.shape
    short = experts % 4 == 0 and experts // 4 <= 4 and 2 * experts <= LANES
    if not (short and shares == 2 and width % (2 * LANES) == 0 and size % 16 == 0):
        return native(
            tokens, cotangent, expert_ids, route_weight, gate_weight, up_weight, down_weight
        )
    grid = Grid(experts)
    me = lax.axis_index("expert")
    half = width // 2
    names = jnp.arange(experts, dtype=jnp.int32)
    named = expert_ids[:, :, None] == names[None, None, :]
    table = jnp.sum(jnp.where(named, route_weight[:, :, None], 0.0), axis=1)
    high = lax.reduce_precision(table, 8, 7)
    extra = jnp.concatenate([high, table - high], axis=1).astype(BF16)
    extra = jnp.pad(extra, ((0, 0), (0, -(2 * experts) % LANES)))
    block = jnp.concatenate([tokens, extra], axis=1)
    token_parts = gather(grid, block, grid.single, True)
    cot_parts = gather(grid, cotangent, grid.single, True)
    gate_w = gate_weight[0]
    up_w = up_weight[0]
    down_w = down_weight[0]
    lanes = jnp.arange(extra.shape[1])[None, :]
    mine = ((lanes % experts) == me) & (lanes < 2 * experts)
    height = experts * size

    def pieces_of(groups, parts):
        arrays, pieces = [], []
        for places, part in zip(groups, parts):
            for q in range(4):
                for i, p in enumerate(places):
                    row = (q * grid.rings + p) * size
                    pieces.append(Piece(len(arrays), row, size, 0, width, i * size))
                arrays.append(part[q])
        return arrays, pieces

    token_arrays, token_pieces = pieces_of(grid.single, token_parts)
    cot_arrays, cot_pieces = pieces_of(grid.single, cot_parts)

    def share_sum(part):
        return plus(part, send(part, [(0, 1), (1, 0)], "dp"))

    def part_of(value, w):
        return jnp.dot(value, w, preferred_element_type=F32)

    all_tokens, weight = assemble(token_arrays, token_pieces, height, width, mine.astype(F32))
    weight = weight[:, :1]
    gate = share_sum(part_of(all_tokens, gate_w).astype(BF16))
    up = share_sum(part_of(all_tokens, up_w).astype(BF16))
    sig = jax.nn.sigmoid(gate)
    hidden = (weight * (gate * sig * up)).astype(BF16)
    hidden, scale = lax.optimization_barrier((hidden, weight))
    (all_cot,) = assemble(cot_arrays, cot_pieces, height, width, None)
    hidden_grad = share_sum((scale * part_of(all_cot, down_w)).astype(BF16))
    up_grad = (hidden_grad * gate * sig).astype(BF16)
    gate_grad = (hidden_grad * up * sig * (1.0 + gate * (1.0 - sig))).astype(BF16)
    contract = (((1,), (1,)), ((), ()))

    def rows_of(value, which):
        runs = []
        for q, p in which:
            start = (q * grid.rings + p) * size
            if runs and runs[-1][1] == start:
                runs[-1][1] = start + size
            else:
                runs.append([start, start + size])
        return rows(*[value[a:b] for a, b in runs])

    def back(value, w, which, side):
        return lax.dot_general(
            rows_of(value, which), w[side * half : (side + 1) * half], contract,
            preferred_element_type=F32,
        )

    def out_part(which, side):
        return back(hidden, down_w, which, side).astype(BF16)

    def grad_part(which, side):
        total = back(gate_grad, gate_w, which, side) + back(up_grad, up_w, which, side)
        return total.astype(BF16)

    mixed = scatter(grid, out_part, grid.together)
    grad_tokens = scatter(grid, grad_part, grid.leaving)
    return (mixed, grad_tokens)


def solution(mesh):
    return jax.shard_map(
        local,
        mesh=mesh,
        in_specs=(
            P("expert", "dp"),
            P("expert", "dp"),
            P("expert", None),
            P("expert", None),
            P("expert", "dp", None),
            P("expert", "dp", None),
            P("expert", "dp", None),
        ),
        out_specs=(P("expert", "dp"), P("expert", "dp")),
        check_vma=False,
    )
```
